1024 devices in a mesh: member: 16 (over y, core), space: 64 (over z, x).
Axes of the slice: x: 4, y: 8, z: 16, core: 2. Of those that a mesh axis runs over, the one named last changes fastest.
Arguments:
- ensemble: float32 [256, 32, 16384], P('member', None, 'space'), may hold values from -6 to 6
- obs_weight: float32 [32, 65536], P(None, 'space'), may hold values from -1 to 1
- obs_value: float32 [65536], P('space'), may hold values from -6 to 6
- obs_rinv: float32 [65536], P('space'), may hold values from 0.5 to 4
- obs_column: int32 [65536], P('space'), may hold values from 0 to 255
- set_rows: int32 [1024, 512], P('space'), may hold values from 0 to 1023
- set_count: int32 [1024], P('space'), may hold values from 128 to 512, as said below
- neighbour: int32 [4, 16384], P(None, 'space'), may hold values from 0 to 15
- interp_weight: float32 [4, 16384], P(None, 'space'), may hold values from 0.1 to 1
Outputs:
- analysed: float32 [256, 32, 16384], P('member', None, 'space')
The draws below stay inside these ranges and needn't reach their ends.
Inputs may be any that keep to these rules, and one draw needn't show every extreme that they name: `set_rows`: a row among the 1024 observations of the space index that owns the coarse point; coarse point j is owned by space index j // (member count). `set_count`: rows of a local set at or past its count are padding; some coarse point has the full 512 rows in every draw. `obs_column`: a column among the 256 columns of the space index that holds the observation. `neighbour`: a coarse point among those owned by the column's own space index, numbered from 0.
All inputs are finite; a program needn't handle non-finite values.
Results may differ from the reference program's by a relative error of at most 0.0035.
Values may be sent and summed in bfloat16 or wider, within the bound.
No kernel may reach another device: no remote copies, remote signals or barrier semaphores. Data moves between devices by JAX's collectives and lax.ppermute only.
A program may use at most 32 MiB of HBM per device.

```python
import math
import jax
import jax.numpy as jnp
from jax import lax

K = 256
NV = 32
LSET = 512
NB = 4
NS_ITERS = 5
COL_DEV = 256
OBS_DEV = 1024
NCOL = 16384
NOBS = 65536
NCP = 1024
N_MEMBER = 16
N_SPACE = 64


def draw_set_count(key, part):
    key_count = jax.random.fold_in(key, 11)
    key_where = jax.random.fold_in(key, 12)
    counts = jax.random.randint(key_count, (NCP,), LSET // 4, LSET + 1)
    where_full = jax.random.randint(key_where, (), 0, NCP)
    return counts.at[where_full].set(LSET).astype(jnp.int32)


def place_ends(result, own_key, smallest, high):
    spot = [jax.random.randint(jax.random.fold_in(own_key, axis), (), 0, length) for axis, length in enumerate(result.shape)]
    longest = result.shape.index(max(result.shape))
    next_to = spot[:longest] + [(spot[longest] + 1) % result.shape[longest]] + spot[longest + 1:]
    return result.at[tuple(spot)].set(smallest).at[tuple(next_to)].set(high)


def block_levels(key, dims, split, smallest, largest):
    loudness, own = 1.0, jax.random.fold_in(key, 6)
    for dim, shards_of in split:
        draws = jnp.exp(jax.random.uniform(jax.random.fold_in(own, dim), (shards_of,), jnp.float32, smallest / len(split), largest / len(split)))
        loudness = loudness * jnp.repeat(draws, dims[dim] // shards_of).reshape([-1 if axis == dim else 1 for axis in range(len(dims))])
    return loudness


def bell_draw(stream_key, extent, scale, limit, shards=(), kind=jnp.bfloat16):
    values = jax.random.normal(stream_key, extent, jnp.float32) * scale
    if len(shards) > 0:
        values = block_levels(stream_key, extent, shards, -0.22, 0.18) * values
    return jnp.clip(values, min=-limit, max=limit).astype(kind)


def setup_inputs(seed: int = 0) -> dict:
    arg_keys = jax.random.split(jax.random.key(seed), 10)
    return {
        "ensemble": bell_draw(arg_keys[0], (K, NV, NCOL), 1.0, 6.0, ((0, 16), (2, 64)), jnp.float32),
        "obs_weight": bell_draw(arg_keys[1], (NV, NOBS), NV ** -0.5, 1.0, ((1, 64),), jnp.float32),
        "obs_value": bell_draw(arg_keys[2], (NOBS,), 1.0, 6.0, ((0, 64),), jnp.float32),
        "obs_rinv": jnp.clip(jnp.exp(math.log(4.0) - 2.0794415 * jax.random.uniform(arg_keys[3], (NOBS,), jnp.float32) ** block_levels(arg_keys[3], (NOBS,), ((0, 64),), -0.2, 0.2)), 0.5, 4.0),
        "obs_column": place_ends(jax.random.randint(arg_keys[4], (NOBS,), 0, COL_DEV), jax.random.fold_in(arg_keys[4], 1), 0, COL_DEV - 1).astype(jnp.int32),
        "set_rows": place_ends(jax.random.randint(arg_keys[5], (NCP, LSET), 0, OBS_DEV), jax.random.fold_in(arg_keys[5], 1), 0, OBS_DEV - 1).astype(jnp.int32),
        "set_count": draw_set_count(jax.random.fold_in(arg_keys[9], 71), 0),
        "neighbour": place_ends(jax.random.randint(arg_keys[7], (NB, NCOL), 0, N_MEMBER), jax.random.fold_in(arg_keys[7], 1), 0, N_MEMBER - 1).astype(jnp.int32),
        "interp_weight": jnp.clip(0.1 + 0.9 * jax.random.uniform(arg_keys[8], (NB, NCOL), jnp.float32) ** block_levels(arg_keys[8], (NB, NCOL), ((1, 64),), -0.2, 0.2), 0.1, 1.0),
    }


highest = lax.Precision.HIGHEST

def make_transform(selected, obs_pick, rinv_pick, count):
    ens_size = selected.shape[0]
    set_len = selected.shape[1]
    obs_mean = lax.optimization_barrier(jnp.mean(selected, axis=0))
    anomaly = selected - obs_mean[None, :]
    innovation = obs_pick - obs_mean
    in_set = jnp.arange(set_len, dtype=jnp.int32) < count
    set_weight = jnp.where(in_set, rinv_pick, jnp.zeros_like(rinv_pick))
    identity = jnp.eye(ens_size, dtype=selected.dtype)
    posterior = (ens_size - 1.0) * identity + jnp.dot(anomaly * set_weight[None, :], anomaly.T, precision=highest)
    frob_norm = jnp.sqrt(jnp.sum(posterior * posterior))
    iterate = posterior / frob_norm
    inverse = identity
    for turn_index in range(NS_ITERS):
        ns_step = 1.5 * identity - 0.5 * jnp.dot(inverse, iterate, precision=highest)
        iterate = jnp.dot(iterate, ns_step, precision=highest)
        inverse = jnp.dot(ns_step, inverse, precision=highest)
    drive_vec = jnp.dot(anomaly, set_weight * innovation, precision=highest)
    mean_weight = jnp.dot(inverse, jnp.dot(inverse, drive_vec, precision=highest), precision=highest) / frob_norm
    spread = inverse * jnp.sqrt((ens_size - 1.0) / frob_norm)
    return (spread + mean_weight[:, None]).astype(jnp.bfloat16)

def reference(ensemble, obs_weight, obs_value, obs_rinv, obs_column, set_rows, set_count, neighbour, interp_weight):
    blocks = N_SPACE
    ens_blocks = ensemble.reshape(K, NV, blocks, COL_DEV).transpose(2, 0, 1, 3)
    weight_blocks = obs_weight.reshape(NV, blocks, OBS_DEV).transpose(1, 0, 2)
    column_blocks = obs_column.reshape(blocks, OBS_DEV)

    def project(operands):
        ens_block, weight_block, column_block = operands
        picked_vals = jnp.take(ens_block, column_block, axis=2)
        return lax.optimization_barrier(jnp.sum(picked_vals * weight_block[None], axis=1))
    observed = lax.map(project, (ens_blocks, weight_blocks, column_blocks))
    value_blocks = obs_value.reshape(blocks, OBS_DEV)
    rinv_blocks = obs_rinv.reshape(blocks, OBS_DEV)

    def analyse(coarse_id):
        block_id = coarse_id // N_MEMBER
        row_ids = set_rows[coarse_id]
        selected = jnp.take(observed[block_id], row_ids, axis=1)
        obs_pick = jnp.take(value_blocks[block_id], row_ids)
        rinv_pick = jnp.take(rinv_blocks[block_id], row_ids)
        return make_transform(selected, obs_pick, rinv_pick, set_count[coarse_id])
    transforms = lax.map(analyse, jnp.arange(NCP, dtype=jnp.int32))
    trans_blocks = transforms.reshape(blocks, N_MEMBER, K, K)
    near_blocks = neighbour.reshape(NB, blocks, COL_DEV).transpose(1, 0, 2)
    interp_blocks = interp_weight.reshape(NB, blocks, COL_DEV).transpose(1, 0, 2)

    def update(operands):
        ens_block, trans_block, near_block, interp_block = operands
        ens_mean = lax.optimization_barrier(jnp.mean(ens_block, axis=0))
        anomalies = (ens_block - ens_mean[None]).astype(jnp.bfloat16)
        norm_weight = interp_block / lax.optimization_barrier(jnp.sum(interp_block, axis=0))[None, :]
        matches = near_block[:, None, :] == jnp.arange(N_MEMBER, dtype=jnp.int32)[None, :, None]
        pointwise = lax.optimization_barrier(jnp.sum(jnp.where(matches, norm_weight[:, None, :], jnp.zeros_like(norm_weight[:, None, :])), axis=0))

        def accumulate(which, running):
            product = jnp.einsum('kl,kvc->lvc', trans_block[which].astype(jnp.float32), anomalies.astype(jnp.float32), precision=highest)
            return running + product * pointwise[which][None, None, :]
        zero_sum = jnp.zeros((K, NV, COL_DEV), dtype=ens_block.dtype)
        return ens_mean[None] + lax.fori_loop(0, N_MEMBER, accumulate, zero_sum)
    analysed = lax.map(update, (ens_blocks, trans_blocks, near_blocks, interp_blocks))
    return analysed.transpose(1, 2, 0, 3).reshape(K, NV, NCOL)
```

```python
import jax
import jax.numpy as jnp
from jax import lax
from jax.experimental import pallas as pl
from jax.experimental.pallas import tpu as pltpu
from jax.sharding import PartitionSpec as P

NS_ITERS = 5
F32 = jnp.float32
BF16 = jnp.bfloat16
VMEM = pl.BlockSpec(memory_space=pltpu.VMEM)
SMEM = pl.BlockSpec(memory_space=pltpu.SMEM)


def split(x):
    hi = x.astype(BF16)
    return hi, (x - hi.astype(F32)).astype(BF16)


def dot(a, b):
    return jnp.dot(a, b, preferred_element_type=F32)


def dot_nt(a, b):
    return lax.dot_general(a, b, (((1,), (1,)), ((), ())), preferred_element_type=F32)


def mm(a, b):
    return dot(a[0], b[0]) + dot(a[0], b[1]) + dot(a[1], b[0])


def pack_kernel(core, ens, mine, theirs):
    half = mine.shape[0]
    own = core[0]
    for v in range(half):
        first = ens[:, v, :].astype(BF16)
        second = ens[:, half + v, :].astype(BF16)
        mine[v] = jnp.where(own == 0, first, second)
        theirs[v] = jnp.where(own == 0, second, first)


def observe_kernel(ens, weight, column, out):
    members, nv, cols = ens.shape
    n_obs = weight.shape[1]
    hi, lo = split(ens[...].reshape(members * nv, cols))
    step = 256
    for start in range(0, n_obs, step):
        at = pl.ds(start, step)
        onehot = (
            lax.broadcasted_iota(jnp.int32, (cols, step), 0) == column[:, at]
        ).astype(F32).astype(BF16)
        picked = dot(hi, onehot) + dot(lo, onehot)
        seen = jnp.sum(picked.reshape(members, nv, step) * weight[:, at][None], axis=1)
        seen = seen.astype(BF16)
        for chip in range(out.shape[0]):
            out[chip, :, at] = seen


def transform_kernel(where, count, mine, theirs, value, rinv, rows, out, obs, left, right):
    chips, per, n_obs = mine.shape
    size = chips * 2 * per
    me, core = where[0], where[1]
    for chip in range(chips):
        obs[pl.ds(pl.multiple_of(2 * per * chip + per * core, per), per), :] = mine[chip].astype(F32)
        obs[pl.ds(pl.multiple_of(2 * per * chip + per * (1 - core), per), per), :] = theirs[chip].astype(F32)
    picks = rows[pl.ds(me, 1), :]
    live = lax.broadcasted_iota(jnp.int32, picks.shape, 1) < count[me]
    picks = jnp.where(live, picks, -1)
    tiles = n_obs // 128
    coarse = lax.broadcasted_iota(jnp.int32, (tiles, picks.shape[1]), 0) == (picks >> 7)
    fine = lax.broadcasted_iota(jnp.int32, (128, picks.shape[1]), 0) == (picks & 127)
    times = dot_nt(coarse.astype(F32).astype(BF16), fine.astype(F32).astype(BF16))
    weight = times * rinv[...]
    for tile in range(tiles):
        at = pl.ds(128 * tile, 128)
        part = obs[:, at]
        mean = jnp.sum(part, axis=0, keepdims=True) * (1.0 / size)
        part = part - mean
        w = weight[tile : tile + 1, :]
        z = w * (value[tile : tile + 1, :] - mean)
        hi, lo = split(part)
        right[0, :, at] = hi
        right[1, :, at] = lo
        hi, lo = split(part * w)
        left[0, :size, at] = hi
        left[1, :size, at] = lo
        hi, lo = split(jnp.broadcast_to(z, (16, 128)))
        left[0, size:, at] = hi
        left[1, size:, at] = lo
    gram = dot_nt(left[0], right[0]) + dot_nt(left[0], right[1]) + dot_nt(left[1], right[0])
    drive = gram[size:]
    diag = lax.broadcasted_iota(jnp.int32, (size, size), 0) == lax.broadcasted_iota(jnp.int32, (size, size), 1)
    eye = diag.astype(F32)
    posterior = gram[:size] + (size - 1.0) * eye
    squares = jnp.sum(jnp.sum(posterior * posterior, axis=0, keepdims=True), axis=1, keepdims=True)
    inv_norm = lax.rsqrt(squares)
    inv_norm = inv_norm * (1.5 - 0.5 * squares * inv_norm * inv_norm)
    product = posterior * inv_norm
    inverse = None
    for turn in range(NS_ITERS):
        ns_step = 1.5 * eye - 0.5 * product
        s = split(ns_step)
        if turn == 0:
            inverse = ns_step
        else:
            inverse = mm(s, split(inverse))
        if turn < NS_ITERS - 1:
            product = mm(s, split(mm(s, split(product))))
    z = split(inverse)
    mean_weight = mm(split(mm(split(drive), z)), z) * inv_norm
    final = inverse * jnp.sqrt((size - 1.0) * inv_norm) + mean_weight[0:1, :]
    final = final.astype(BF16)
    for chip in range(chips):
        block = final[2 * per * chip : 2 * per * (chip + 1)]
        out[2 * chip] = block
        out[2 * chip + 1] = block


def apply_kernel(where, trans, neighbour, interp, *refs):
    blocks, (keep, send, lhs, x) = refs[:-4], refs[-4:]
    points, rows, size = trans.shape
    half, per = keep.shape[1], keep.shape[0]
    cols = keep.shape[2]
    chip, core = where[2], where[1]
    chips = size // (2 * per)
    raw = interp[...]
    norm = raw / jnp.sum(raw, axis=0, keepdims=True)
    near = neighbour[...]
    point = lax.broadcasted_iota(jnp.int32, (points, cols), 0)
    pointwise = jnp.zeros((points, cols), F32)
    for b in range(raw.shape[0]):
        pointwise = pointwise + jnp.where(point == near[b : b + 1], norm[b : b + 1], 0.0)
    flat = trans[...].reshape(points * rows, size)
    lhs[: points * rows] = flat
    lhs[points * rows :] = jnp.full((16, size), 1.0 / size, BF16)
    sums = jnp.sum(flat.astype(F32), axis=1, keepdims=True)
    rest = jnp.ones((rows, cols), F32)
    for m in range(points):
        rest = rest - sums[rows * m : rows * (m + 1)] * pointwise[m : m + 1]
    for v in range(half):
        slot = v % 2
        for (shift, rel), block in blocks_of(blocks):
            src = lax.rem(chip + shift + chips, chips)
            at = pl.multiple_of(2 * per * src + per * (core if rel == 0 else 1 - core), per)
            x[slot, pl.ds(at, per), :] = block[v] if rel is None or len(block.shape) == 3 else block[rel, v]
        res = dot(lhs[...], x[slot])
        total = res[points * rows : points * rows + 1] * rest
        for m in range(points):
            total = total + res[rows * m : rows * (m + 1)] * pointwise[m : m + 1]
        low, high = total[:per], total[per:]
        keep[:, v, :] = jnp.where(core == 0, low, high)
        send[:, v, :] = jnp.where(core == 0, high, low)


def blocks_of(blocks):
    for block, shift in zip(blocks[:7], (0, -1, 1, -2, 2, -3, 3)):
        yield (shift, 0), block
        yield (shift, 1), block
    yield (-4, 0), blocks[7]
    yield (4, 1), blocks[8]


def local(ensemble, obs_weight, obs_value, obs_rinv, obs_column, set_rows, set_count, neighbour, interp_weight):
    count = lax.axis_size("member")
    chips = count // 2
    me = lax.axis_index("member").astype(jnp.int32)
    core = me % 2
    where = jnp.stack([me, core, me // 2])
    per, nv, cols = ensemble.shape
    half = nv // 2
    n_obs = obs_column.shape[0]
    swap = [(i, i ^ 1) for i in range(count)]
    up = [(i, (i + 2) % count) for i in range(count)]
    down = [(i, (i - 2) % count) for i in range(count)]
    same_core = [[2 * y + c for y in range(chips)] for c in range(2)]

    piece = jax.ShapeDtypeStruct((half, per, cols), BF16)
    mine, theirs = pl.pallas_call(
        pack_kernel, out_shape=(piece, piece), in_specs=[SMEM, VMEM], out_specs=(VMEM, VMEM), name="pack"
    )(core.reshape(1), ensemble)
    theirs = lax.ppermute(theirs, "member", swap)
    seen = pl.pallas_call(
        observe_kernel,
        out_shape=jax.ShapeDtypeStruct((chips, per, n_obs), BF16),
        in_specs=[VMEM] * 3,
        out_specs=VMEM,
        name="observe",
    )(ensemble, obs_weight, obs_column.reshape(1, n_obs))
    seen = lax.all_to_all(seen, "member", 0, 0, axis_index_groups=same_core, tiled=True)
    seen_too = lax.ppermute(seen, "member", swap)

    own = jnp.stack([mine, theirs])
    blocks = [own]
    from_below, from_above = own, own
    for hop in range(3):
        from_below = lax.ppermute(from_below, "member", up)
        from_above = lax.ppermute(from_above, "member", down)
        blocks += [from_below, from_above]
    blocks += [lax.ppermute(from_below[0], "member", up), lax.ppermute(from_above[1], "member", down)]

    trans = pl.pallas_call(
        transform_kernel,
        out_shape=jax.ShapeDtypeStruct((count, 2 * per, count * per), BF16),
        in_specs=[SMEM, SMEM] + [VMEM] * 5,
        out_specs=VMEM,
        scratch_shapes=[
            pltpu.VMEM((count * per, n_obs), F32),
            pltpu.VMEM((2, count * per + 16, n_obs), BF16),
            pltpu.VMEM((2, count * per, n_obs), BF16),
        ],
        name="transform",
    )(
        where,
        set_count,
        seen,
        seen_too,
        obs_value.reshape(n_obs // 128, 128),
        obs_rinv.reshape(n_obs // 128, 128),
        set_rows,
    )
    trans = lax.all_to_all(trans, "member", 0, 0, tiled=True)

    part = jax.ShapeDtypeStruct((per, half, cols), F32)
    keep, send = pl.pallas_call(
        apply_kernel,
        out_shape=(part, part),
        in_specs=[SMEM] + [VMEM] * (3 + len(blocks)),
        out_specs=(VMEM, VMEM),
        scratch_shapes=[
            pltpu.VMEM((count * 2 * per + 16, count * per), BF16),
            pltpu.VMEM((2, count * per, cols), BF16),
        ],
        name="apply",
    )(where, trans, neighbour, interp_weight, *blocks)
    other = lax.ppermute(send, "member", swap)
    return jnp.where(
        core == 0, jnp.concatenate([keep, other], axis=1), jnp.concatenate([other, keep], axis=1)
    )


def solution(mesh):
    placed = (
        P("member", None, "space"),
        P(None, "space"),
        P("space"),
        P("space"),
        P("space"),
        P("space", None),
        P("space"),
        P(None, "space"),
        P(None, "space"),
    )
    return jax.shard_map(
        local, mesh=mesh, in_specs=placed, out_specs=P("member", None, "space"), check_vma=False
    )
```

```python
import jax
import jax.numpy as jnp
from jax import lax
from jax.experimental import pallas as pl
from jax.experimental.pallas import tpu as pltpu
from jax.sharding import PartitionSpec as P


NS_ITERS = 5
F32 = jnp.float32
BF16 = jnp.bfloat16
VMEM = pl.BlockSpec(memory_space=pltpu.VMEM)
SMEM = pl.BlockSpec(memory_space=pltpu.SMEM)


def limit(mib):
    return pltpu.CompilerParams(vmem_limit_bytes=mib << 20)


def split(x):
    hi = x.astype(BF16)
    return hi, (x - hi.astype(F32)).astype(BF16)


def dot(a, b):
    return jnp.dot(a, b, preferred_element_type=F32)


def dot_nt(a, b):
    return lax.dot_general(a, b, (((1,), (1,)), ((), ())), preferred_element_type=F32)


def mm(a, b):
    return dot(a[0], b[0]) + dot(a[0], b[1]) + dot(a[1], b[0])


def pack_kernel(ens, out):
    for v in range(out.shape[0]):
        out[v] = ens[:, v, :].astype(BF16)


def observe_kernel(ens, weight, column, out):
    members, nv, cols = ens.shape
    n_obs = weight.shape[1]
    hi, lo = split(ens[...].reshape(members * nv, cols))
    step = 256
    for start in range(0, n_obs, step):
        at = pl.ds(start, step)
        onehot = (
            lax.broadcasted_iota(jnp.int32, (cols, step), 0) == column[:, at]
        ).astype(F32).astype(BF16)
        picked = dot(hi, onehot) + dot(lo, onehot)
        seen = jnp.sum(picked.reshape(members, nv, step) * weight[:, at][None], axis=1)
        seen = seen.astype(BF16)
        for chip in range(out.shape[0]):
            out[chip, :, at] = seen


def transform_kernel(where, mine, theirs, value, rinv, rows, counts, out, obs, scaled):
    chips, per, n_obs = mine.shape
    size = chips * 2 * per
    me, core = where[0], where[1]
    for chip in range(chips):
        obs[pl.ds(pl.multiple_of(2 * per * chip + per * core, per), per), :] = mine[chip]
        obs[pl.ds(pl.multiple_of(2 * per * chip + per * (1 - core), per), per), :] = theirs[chip]
    picks = rows[pl.ds(me, 1), :]
    mine_only = lax.broadcasted_iota(jnp.int32, counts.shape, 1) == me
    count = jnp.sum(jnp.where(mine_only, counts[...].astype(F32), 0.0), axis=1, keepdims=True)
    live = lax.broadcasted_iota(jnp.int32, picks.shape, 1).astype(F32) < count
    picks = jnp.where(live, picks, -1)
    tiles = n_obs // 128
    coarse = lax.broadcasted_iota(jnp.int32, (tiles, picks.shape[1]), 0) == (picks >> 7)
    fine = lax.broadcasted_iota(jnp.int32, (128, picks.shape[1]), 0) == (picks & 127)
    times = dot_nt(coarse.astype(F32).astype(BF16), fine.astype(F32).astype(BF16))
    root = jnp.sqrt(times * rinv[...])
    for tile in range(tiles):
        at = pl.ds(128 * tile, 128)
        part = obs[:, at].astype(F32)
        mean = jnp.sum(part, axis=0, keepdims=True) * (1.0 / size)
        w = root[tile : tile + 1, :]
        z = w * (value[tile : tile + 1, :] - mean)
        hi, lo = split((part - mean) * w)
        scaled[0, :size, at] = hi
        scaled[1, :size, at] = lo
        hi, lo = split(jnp.broadcast_to(z, (16, 128)))
        scaled[0, size:, at] = hi
        scaled[1, size:, at] = lo
    hi, lo = scaled[0], scaled[1]
    gram = dot_nt(hi, hi[:size]) + dot_nt(hi, lo[:size]) + dot_nt(lo, hi[:size])
    drive = gram[size:]
    diag = lax.broadcasted_iota(jnp.int32, (size, size), 0) == lax.broadcasted_iota(jnp.int32, (size, size), 1)
    eye = diag.astype(F32)
    posterior = gram[:size] + (size - 1.0) * eye
    squares = jnp.sum(jnp.sum(posterior * posterior, axis=0, keepdims=True), axis=1, keepdims=True)
    inv_norm = lax.rsqrt(squares)
    inv_norm = inv_norm * (1.5 - 0.5 * squares * inv_norm * inv_norm)
    product = posterior * inv_norm
    inverse = None
    for turn in range(NS_ITERS):
        ns_step = 1.5 * eye - 0.5 * product
        s = split(ns_step)
        if turn == 0:
            inverse = ns_step
        else:
            inverse = mm(s, split(inverse))
        if turn < NS_ITERS - 1:
            product = mm(s, split(mm(s, split(product))))
    z = split(inverse)
    mean_weight = mm(split(mm(split(drive), z)), z) * inv_norm
    final = inverse * jnp.sqrt((size - 1.0) * inv_norm) + mean_weight[0:1, :]
    final = final.astype(BF16)
    for to in range(2 * chips):
        out[to] = final[per * to : per * (to + 1)]


def apply_kernel(where, trans, neighbour, interp, *refs):
    blocks, (out, lhs) = refs[:-2], refs[-2:]
    points, per, size = trans.shape
    nv, cols = out.shape[1:]
    core, chip = where[1], where[2]
    chips = size // (2 * per)
    raw = interp[...]
    norm = raw / jnp.sum(raw, axis=0, keepdims=True)
    near = neighbour[...]
    point = lax.broadcasted_iota(jnp.int32, (points, cols), 0)
    pointwise = jnp.zeros((points, cols), F32)
    for b in range(raw.shape[0]):
        pointwise = pointwise + jnp.where(point == near[b : b + 1], norm[b : b + 1], 0.0)
    flat = trans[...].reshape(points * per, size)
    sums = jnp.sum(flat.astype(F32), axis=1, keepdims=True)
    rest = jnp.ones((per, cols), F32)
    for m in range(points):
        rest = rest - sums[per * m : per * (m + 1)] * pointwise[m : m + 1]
    lane = lax.broadcasted_iota(jnp.int32, (1, size), 1)
    column = lane % per
    ahead = 2 * core - 1
    for place, (_, _, steps, other) in enumerate(slabs()):
        src = lax.rem(chip + ahead * steps + chips, chips)
        start = per * (2 * src + (1 - core if other else core))
        column = column + jnp.where(lane // per == place, start, 0)
    shuffle = (lax.broadcasted_iota(jnp.int32, (size, size), 0) == column).astype(F32).astype(BF16)
    lhs[: points * per] = dot(flat, shuffle).astype(BF16)
    lhs[points * per :] = jnp.full((16, size), 1.0 / size, BF16)
    for v in range(nv):
        states = jnp.concatenate(
            [blocks[which][v] if index is None else blocks[which][index, v] for which, index, _, _ in slabs()], axis=0
        )
        res = dot(lhs[...], states)
        total = res[points * per : points * per + 1] * rest
        for m in range(points):
            total = total + res[per * m : per * (m + 1)] * pointwise[m : m + 1]
        out[:, v, :] = total


def slabs():
    for hop in range(4):
        yield hop, 0, hop, False
        yield hop, 1, hop, True
    for hop in (1, 2, 3):
        yield 3 + hop, 0, -hop, True
        yield 3 + hop, 1, -hop, False
    yield 7, None, 4, False
    yield 8, None, 4, True


def permute(value, pairs):
    return lax.ppermute(value, "member", pairs)


def analysis(ensemble, obs_weight, obs_value, obs_rinv, obs_column, set_rows, set_count, neighbour, interp_weight):
    count = lax.axis_size("member")
    chips = count // 2
    me = lax.axis_index("member").astype(jnp.int32)
    core = me % 2
    where = jnp.stack([me, core, me // 2])
    per, nv, cols = ensemble.shape
    n_obs = obs_column.shape[0]
    swap = [(i, i ^ 1) for i in range(count)]
    same_core = [[2 * y + c for y in range(chips)] for c in range(2)]

    def along(hops):
        return [(2 * y + c, 2 * ((y + (hops if c else -hops) * -1) % chips) + c) for y in range(chips) for c in range(2)]

    mine = pl.pallas_call(
        pack_kernel,
        out_shape=jax.ShapeDtypeStruct((nv, per, cols), BF16),
        in_specs=[VMEM],
        out_specs=VMEM,
        compiler_params=limit(4),
        name="pack",
    )(ensemble)
    theirs = permute(mine, swap)
    own = jnp.stack([mine, theirs])
    first = permute(own, along(1))
    second = permute(first, along(1))
    third = permute(second, along(1))
    far = permute(first[0], along(3))
    first_too = permute(first, swap)
    second_too = permute(second, swap)
    third_too = permute(third, swap)
    far_too = permute(far, swap)
    blocks = [own, first, second, third, first_too, second_too, third_too, far, far_too]

    seen = pl.pallas_call(
        observe_kernel,
        out_shape=jax.ShapeDtypeStruct((chips, per, n_obs), BF16),
        in_specs=[VMEM] * 3,
        out_specs=VMEM,
        compiler_params=limit(8),
        name="observe",
    )(ensemble, obs_weight, obs_column.reshape(1, n_obs))
    seen = lax.all_to_all(seen, "member", 0, 0, axis_index_groups=same_core, tiled=True)
    seen_too = permute(seen, swap)

    trans = pl.pallas_call(
        transform_kernel,
        out_shape=jax.ShapeDtypeStruct((count, per, count * per), BF16),
        in_specs=[SMEM] + [VMEM] * 6,
        out_specs=VMEM,
        scratch_shapes=[
            pltpu.VMEM((count * per, n_obs), BF16),
            pltpu.VMEM((2, count * per + 16, n_obs), BF16),
        ],
        compiler_params=limit(8),
        name="transform",
    )(
        where,
        seen,
        seen_too,
        obs_value.reshape(n_obs // 128, 128),
        obs_rinv.reshape(n_obs // 128, 128),
        set_rows,
        set_count.reshape(1, count),
    )
    trans = lax.all_to_all(trans, "member", 0, 0, tiled=True)

    return pl.pallas_call(
        apply_kernel,
        out_shape=jax.ShapeDtypeStruct((per, nv, cols), F32),
        in_specs=[SMEM] + [VMEM] * (3 + len(blocks)),
        out_specs=VMEM,
        scratch_shapes=[
            pltpu.VMEM((count * per + 16, count * per), BF16),
        ],
        compiler_params=limit(4),
        name="apply",
    )(where, trans, neighbour, interp_weight, *blocks)


def solution(mesh):
    placed = (
        P("member", None, "space"),
        P(None, "space"),
        P("space"),
        P("space"),
        P("space"),
        P("space", None),
        P("space"),
        P(None, "space"),
        P(None, "space"),
    )
    return jax.shard_map(
        analysis, mesh=mesh, in_specs=placed, out_specs=P("member", None, "space"), check_vma=False
    )
```

```python
import jax
import jax.numpy as jnp
from jax import lax
from jax.experimental import pallas as pl
from jax.experimental.pallas import tpu as pltpu
from jax.sharding import PartitionSpec as P


NS_ITERS = 5
F32 = jnp.float32
BF16 = jnp.bfloat16
VMEM = pl.BlockSpec(memory_space=pltpu.VMEM)
SMEM = pl.BlockSpec(memory_space=pltpu.SMEM)


def limit(mib):
    return pltpu.CompilerParams(vmem_limit_bytes=mib << 20)


def split(x):
    hi = x.astype(BF16)
    return hi, (x - hi.astype(F32)).astype(BF16)


def dot(a, b):
    return jnp.dot(a, b, preferred_element_type=F32)


def dot_nt(a, b):
    return lax.dot_general(a, b, (((1,), (1,)), ((), ())), preferred_element_type=F32)


def mm(a, b):
    return dot(a[0], b[0]) + dot(a[0], b[1]) + dot(a[1], b[0])


def pack_kernel(ens, out):
    for v in range(out.shape[0]):
        out[v] = ens[:, v, :].astype(BF16)


def observe_kernel(ens, weight, column, out):
    members, nv, cols = ens.shape
    n_obs = weight.shape[1]
    hi, lo = split(ens[...].reshape(members * nv, cols))
    step = 256
    for start in range(0, n_obs, step):
        at = pl.ds(start, step)
        onehot = (
            lax.broadcasted_iota(jnp.int32, (cols, step), 0) == column[:, at]
        ).astype(F32).astype(BF16)
        picked = dot(hi, onehot) + dot(lo, onehot)
        seen = jnp.sum(picked.reshape(members, nv, step) * weight[:, at][None], axis=1)
        seen = seen.astype(BF16)
        for chip in range(out.shape[0]):
            out[chip, :, at] = seen


def transform_kernel(where, mine, theirs, value, rinv, rows, out, obs, scaled):
    chips, per, n_obs = mine.shape
    size = chips * 2 * per
    me, core = where[0], where[1]
    for chip in range(chips):
        obs[pl.ds(pl.multiple_of(2 * per * chip + per * core, per), per), :] = mine[chip]
        obs[pl.ds(pl.multiple_of(2 * per * chip + per * (1 - core), per), per), :] = theirs[chip]
    picks = rows[pl.ds(me, 1), :]
    live = lax.broadcasted_iota(jnp.int32, picks.shape, 1) < where[3 + me]
    picks = jnp.where(live, picks, -1)
    tiles = n_obs // 128
    coarse = lax.broadcasted_iota(jnp.int32, (tiles, picks.shape[1]), 0) == (picks >> 7)
    fine = lax.broadcasted_iota(jnp.int32, (128, picks.shape[1]), 0) == (picks & 127)
    times = dot_nt(coarse.astype(F32).astype(BF16), fine.astype(F32).astype(BF16))
    root = jnp.sqrt(times * rinv[...])
    for tile in range(tiles):
        at = pl.ds(128 * tile, 128)
        part = obs[:, at].astype(F32)
        mean = jnp.sum(part, axis=0, keepdims=True) * (1.0 / size)
        w = root[tile : tile + 1, :]
        z = w * (value[tile : tile + 1, :] - mean)
        hi, lo = split((part - mean) * w)
        scaled[0, :size, at] = hi
        scaled[1, :size, at] = lo
        hi, lo = split(jnp.broadcast_to(z, (16, 128)))
        scaled[0, size:, at] = hi
        scaled[1, size:, at] = lo
    hi, lo = scaled[0], scaled[1]
    gram = dot_nt(hi, hi[:size]) + dot_nt(hi, lo[:size]) + dot_nt(lo, hi[:size])
    drive = gram[size:]
    diag = lax.broadcasted_iota(jnp.int32, (size, size), 0) == lax.broadcasted_iota(jnp.int32, (size, size), 1)
    eye = diag.astype(F32)
    posterior = gram[:size] + (size - 1.0) * eye
    squares = jnp.sum(jnp.sum(posterior * posterior, axis=0, keepdims=True), axis=1, keepdims=True)
    inv_norm = lax.rsqrt(squares)
    inv_norm = inv_norm * (1.5 - 0.5 * squares * inv_norm * inv_norm)
    product = posterior * inv_norm
    inverse = None
    for turn in range(NS_ITERS):
        ns_step = 1.5 * eye - 0.5 * product
        s = split(ns_step)
        if turn == 0:
            inverse = ns_step
        else:
            inverse = mm(s, split(inverse))
        if turn < NS_ITERS - 1:
            product = mm(s, split(mm(s, split(product))))
    z = split(inverse)
    mean_weight = mm(split(mm(split(drive), z)), z) * inv_norm
    final = inverse * jnp.sqrt((size - 1.0) * inv_norm) + mean_weight[0:1, :]
    final = final.astype(BF16)
    for to in range(2 * chips):
        out[to] = final[per * to : per * (to + 1)]


def apply_kernel(where, trans, neighbour, interp, *refs):
    blocks, (out, lhs) = refs[:-2], refs[-2:]
    points, per, size = trans.shape
    nv, cols = out.shape[1:]
    core, chip = where[1], where[2]
    chips = size // (2 * per)
    raw = interp[...]
    norm = raw / jnp.sum(raw, axis=0, keepdims=True)
    near = neighbour[...]
    point = lax.broadcasted_iota(jnp.int32, (points, cols), 0)
    pointwise = jnp.zeros((points, cols), F32)
    for b in range(raw.shape[0]):
        pointwise = pointwise + jnp.where(point == near[b : b + 1], norm[b : b + 1], 0.0)
    flat = trans[...].reshape(points * per, size)
    sums = jnp.sum(flat.astype(F32), axis=1, keepdims=True)
    rest = jnp.ones((per, cols), F32)
    for m in range(points):
        rest = rest - sums[per * m : per * (m + 1)] * pointwise[m : m + 1]
    lane = lax.broadcasted_iota(jnp.int32, (1, size), 1)
    column = lane % per
    ahead = 2 * core - 1
    for place, (_, _, steps, other) in enumerate(slabs()):
        src = lax.rem(chip + ahead * steps + chips, chips)
        start = per * (2 * src + (1 - core if other else core))
        column = column + jnp.where(lane // per == place, start, 0)
    shuffle = (lax.broadcasted_iota(jnp.int32, (size, size), 0) == column).astype(F32).astype(BF16)
    lhs[: points * per] = dot(flat, shuffle).astype(BF16)
    lhs[points * per :] = jnp.full((16, size), 1.0 / size, BF16)
    for v in range(nv):
        states = jnp.concatenate(
            [blocks[which][v] if index is None else blocks[which][index, v] for which, index, _, _ in slabs()], axis=0
        )
        res = dot(lhs[...], states)
        total = res[points * per : points * per + 1] * rest
        for m in range(points):
            total = total + res[per * m : per * (m + 1)] * pointwise[m : m + 1]
        out[:, v, :] = total


def slabs():
    for hop in range(4):
        yield hop, 0, hop, False
        yield hop, 1, hop, True
    for hop in (1, 2, 3):
        yield 3 + hop, 0, -hop, True
        yield 3 + hop, 1, -hop, False
    yield 7, None, 4, False
    yield 8, None, 4, True


def permute(value, pairs):
    return lax.ppermute(value, "member", pairs)


def analysis(ensemble, obs_weight, obs_value, obs_rinv, obs_column, set_rows, set_count, neighbour, interp_weight):
    count = lax.axis_size("member")
    chips = count // 2
    me = lax.axis_index("member").astype(jnp.int32)
    core = me % 2
    where = jnp.concatenate([jnp.stack([me, core, me // 2]), set_count])
    per, nv, cols = ensemble.shape
    n_obs = obs_column.shape[0]
    swap = [(i, i ^ 1) for i in range(count)]
    same_core = [[2 * y + c for y in range(chips)] for c in range(2)]

    def along(hops):
        return [(2 * y + c, 2 * ((y + (hops if c else -hops) * -1) % chips) + c) for y in range(chips) for c in range(2)]

    mine = pl.pallas_call(
        pack_kernel,
        out_shape=jax.ShapeDtypeStruct((nv, per, cols), BF16),
        in_specs=[VMEM],
        out_specs=VMEM,
        compiler_params=limit(4),
        name="pack",
    )(ensemble)
    theirs = permute(mine, swap)
    own = jnp.stack([mine, theirs])
    first = permute(own, along(1))
    second = permute(first, along(1))
    third = permute(second, along(1))
    far = permute(first[0], along(3))
    first_too = permute(first, swap)
    second_too = permute(second, swap)
    third_too = permute(third, swap)
    far_too = permute(far, swap)
    blocks = [own, first, second, third, first_too, second_too, third_too, far, far_too]

    seen = pl.pallas_call(
        observe_kernel,
        out_shape=jax.ShapeDtypeStruct((chips, per, n_obs), BF16),
        in_specs=[VMEM] * 3,
        out_specs=VMEM,
        compiler_params=limit(8),
        name="observe",
    )(ensemble, obs_weight, obs_column.reshape(1, n_obs))
    seen = lax.all_to_all(seen, "member", 0, 0, axis_index_groups=same_core, tiled=True)
    seen_too = permute(seen, swap)

    trans = pl.pallas_call(
        transform_kernel,
        out_shape=jax.ShapeDtypeStruct((count, per, count * per), BF16),
        in_specs=[SMEM] + [VMEM] * 5,
        out_specs=VMEM,
        scratch_shapes=[
            pltpu.VMEM((count * per, n_obs), BF16),
            pltpu.VMEM((2, count * per + 16, n_obs), BF16),
        ],
        compiler_params=limit(8),
        name="transform",
    )(
        where,
        seen,
        seen_too,
        obs_value.reshape(n_obs // 128, 128),
        obs_rinv.reshape(n_obs // 128, 128),
        set_rows,
    )
    trans = lax.all_to_all(trans, "member", 0, 0, tiled=True)

    return pl.pallas_call(
        apply_kernel,
        out_shape=jax.ShapeDtypeStruct((per, nv, cols), F32),
        in_specs=[SMEM] + [VMEM] * (3 + len(blocks)),
        out_specs=VMEM,
        scratch_shapes=[
            pltpu.VMEM((count * per + 16, count * per), BF16),
        ],
        compiler_params=limit(4),
        name="apply",
    )(where, trans, neighbour, interp_weight, *blocks)


def solution(mesh):
    placed = (
        P("member", None, "space"),
        P(None, "space"),
        P("space"),
        P("space"),
        P("space"),
        P("space", None),
        P("space"),
        P(None, "space"),
        P(None, "space"),
    )
    return jax.shard_map(
        analysis, mesh=mesh, in_specs=placed, out_specs=P("member", None, "space"), check_vma=False
    )
```

```python
import jax
import jax.numpy as jnp
from jax import lax
from jax.experimental import pallas as pl
from jax.experimental.pallas import tpu as pltpu
from jax.sharding import PartitionSpec as P


NS_ITERS = 5
F32 = jnp.float32
BF16 = jnp.bfloat16
VMEM = pl.BlockSpec(memory_space=pltpu.VMEM)
SMEM = pl.BlockSpec(memory_space=pltpu.SMEM)


def limit(mib):
    return pltpu.CompilerParams(vmem_limit_bytes=mib << 20)


def split(x):
    hi = x.astype(BF16)
    return hi, (x - hi.astype(F32)).astype(BF16)


def dot(a, b):
    return jnp.dot(a, b, preferred_element_type=F32)


def dot_nt(a, b):
    return lax.dot_general(a, b, (((1,), (1,)), ((), ())), preferred_element_type=F32)


def mm(a, b):
    return dot(a[0], b[0]) + dot(a[0], b[1]) + dot(a[1], b[0])


def pack_kernel(ens, out):
    for v in range(out.shape[0]):
        out[v] = ens[:, v, :].astype(BF16)


def observe_kernel(ens, weight, column, out):
    members, nv, cols = ens.shape
    n_obs = weight.shape[1]
    hi, lo = split(ens[...].reshape(members * nv, cols))
    step = 256
    for start in range(0, n_obs, step):
        at = pl.ds(start, step)
        onehot = (
            lax.broadcasted_iota(jnp.int32, (cols, step), 0) == column[:, at]
        ).astype(F32).astype(BF16)
        picked = dot(hi, onehot) + dot(lo, onehot)
        seen = jnp.sum(picked.reshape(members, nv, step) * weight[:, at][None], axis=1)
        seen = seen.astype(BF16)
        for chip in range(out.shape[0]):
            out[chip, :, at] = seen


def transform_kernel(where, mine, theirs, value, rinv, rows, out, obs, scaled):
    chips, per, n_obs = mine.shape
    size = chips * 2 * per
    me, core = where[0], where[1]
    for chip in range(chips):
        obs[pl.ds(pl.multiple_of(2 * per * chip + per * core, per), per), :] = mine[chip]
        obs[pl.ds(pl.multiple_of(2 * per * chip + per * (1 - core), per), per), :] = theirs[chip]
    picks = rows[pl.ds(me, 1), :]
    live = lax.broadcasted_iota(jnp.int32, picks.shape, 1) < where[3 + me]
    picks = jnp.where(live, picks, -1)
    tiles = n_obs // 128
    coarse = lax.broadcasted_iota(jnp.int32, (tiles, picks.shape[1]), 0) == (picks >> 7)
    fine = lax.broadcasted_iota(jnp.int32, (128, picks.shape[1]), 0) == (picks & 127)
    times = dot_nt(coarse.astype(F32).astype(BF16), fine.astype(F32).astype(BF16))
    root = jnp.sqrt(times * rinv[...])
    for tile in range(tiles):
        at = pl.ds(128 * tile, 128)
        part = obs[:, at].astype(F32)
        mean = jnp.sum(part, axis=0, keepdims=True) * (1.0 / size)
        w = root[tile : tile + 1, :]
        z = w * (value[tile : tile + 1, :] - mean)
        hi, lo = split((part - mean) * w)
        scaled[0, :size, at] = hi
        scaled[1, :size, at] = lo
        hi, lo = split(jnp.broadcast_to(z, (16, 128)))
        scaled[0, size:, at] = hi
        scaled[1, size:, at] = lo
    hi, lo = scaled[0], scaled[1]
    gram = dot_nt(hi, hi[:size]) + dot_nt(hi, lo[:size]) + dot_nt(lo, hi[:size])
    drive = gram[size:]
    diag = lax.broadcasted_iota(jnp.int32, (size, size), 0) == lax.broadcasted_iota(jnp.int32, (size, size), 1)
    eye = diag.astype(F32)
    posterior = gram[:size] + (size - 1.0) * eye
    squares = jnp.sum(jnp.sum(posterior * posterior, axis=0, keepdims=True), axis=1, keepdims=True)
    inv_norm = lax.rsqrt(squares)
    inv_norm = inv_norm * (1.5 - 0.5 * squares * inv_norm * inv_norm)
    product = posterior * inv_norm
    inverse = None
    for turn in range(NS_ITERS):
        ns_step = 1.5 * eye - 0.5 * product
        s = split(ns_step)
        if turn == 0:
            inverse = ns_step
        else:
            inverse = mm(s, split(inverse))
        if turn < NS_ITERS - 1:
            product = mm(s, split(mm(s, split(product))))
    z = split(inverse)
    mean_weight = mm(split(mm(split(drive), z)), z) * inv_norm
    final = inverse * jnp.sqrt((size - 1.0) * inv_norm) + mean_weight[0:1, :]
    final = final.astype(BF16)
    for to in range(2 * chips):
        out[to] = final[per * to : per * (to + 1)]


def apply_kernel(where, trans, neighbour, interp, *refs):
    blocks, (out, lhs, held, sems) = refs[:-4], refs[-4:]
    points, per, size = trans.shape
    nv, cols = held.shape[1:]
    core, chip = where[1], where[2]
    chips = size // (2 * per)
    raw = interp[...]
    norm = raw / jnp.sum(raw, axis=0, keepdims=True)
    near = neighbour[...]
    point = lax.broadcasted_iota(jnp.int32, (points, cols), 0)
    pointwise = jnp.zeros((points, cols), F32)
    for b in range(raw.shape[0]):
        pointwise = pointwise + jnp.where(point == near[b : b + 1], norm[b : b + 1], 0.0)
    flat = trans[...].reshape(points * per, size)
    sums = jnp.sum(flat.astype(F32), axis=1, keepdims=True)
    rest = jnp.ones((per, cols), F32)
    for m in range(points):
        rest = rest - sums[per * m : per * (m + 1)] * pointwise[m : m + 1]
    lane = lax.broadcasted_iota(jnp.int32, (1, size), 1)
    column = lane % per
    ahead = 2 * core - 1
    for place, (_, _, steps, other) in enumerate(slabs()):
        src = lax.rem(chip + ahead * steps + chips, chips)
        start = per * (2 * src + (1 - core if other else core))
        column = column + jnp.where(lane // per == place, start, 0)
    shuffle = (lax.broadcasted_iota(jnp.int32, (size, size), 0) == column).astype(F32).astype(BF16)
    lhs[: points * per] = dot(flat, shuffle).astype(BF16)
    lhs[points * per :] = jnp.full((16, size), 1.0 / size, BF16)
    each, copies = nv // sems.shape[0], []
    for v in range(nv):
        states = jnp.concatenate(
            [blocks[which][v] if index is None else blocks[which][index, v] for which, index, _, _ in slabs()], axis=0
        )
        res = dot(lhs[...], states)
        total = res[points * per : points * per + 1] * rest
        for m in range(points):
            total = total + res[per * m : per * (m + 1)] * pointwise[m : m + 1]
        held[:, v, :] = total
        if (v + 1) % each == 0:
            at = pl.ds(v + 1 - each, each)
            copies.append(pltpu.make_async_copy(held.at[:, at], out.at[:, at], sems.at[len(copies)]))
            copies[-1].start()
    for copy in copies:
        copy.wait()


def slabs():
    for hop in range(4):
        yield hop, 0, hop, False
        yield hop, 1, hop, True
    for hop in (1, 2, 3):
        yield 3 + hop, 0, -hop, True
        yield 3 + hop, 1, -hop, False
    yield 7, None, 4, False
    yield 8, None, 4, True


def permute(value, pairs):
    return lax.ppermute(value, "member", pairs)


def analysis(ensemble, obs_weight, obs_value, obs_rinv, obs_column, set_rows, set_count, neighbour, interp_weight):
    count = lax.axis_size("member")
    chips = count // 2
    me = lax.axis_index("member").astype(jnp.int32)
    core = me % 2
    where = jnp.concatenate([jnp.stack([me, core, me // 2]), set_count])
    per, nv, cols = ensemble.shape
    n_obs = obs_column.shape[0]
    swap = [(i, i ^ 1) for i in range(count)]
    same_core = [[2 * y + c for y in range(chips)] for c in range(2)]

    def along(hops):
        return [(2 * y + c, 2 * ((y + (hops if c else -hops) * -1) % chips) + c) for y in range(chips) for c in range(2)]

    mine = pl.pallas_call(
        pack_kernel,
        out_shape=jax.ShapeDtypeStruct((nv, per, cols), BF16),
        in_specs=[VMEM],
        out_specs=VMEM,
        compiler_params=limit(4),
        name="pack",
    )(ensemble)
    theirs = permute(mine, swap)
    own = jnp.stack([mine, theirs])
    first = permute(own, along(1))
    second = permute(first, along(1))
    third = permute(second, along(1))
    far = permute(first[0], along(3))
    first_too = permute(first, swap)
    second_too = permute(second, swap)
    third_too = permute(third, swap)
    far_too = permute(far, swap)
    blocks = [own, first, second, third, first_too, second_too, third_too, far, far_too]

    seen = pl.pallas_call(
        observe_kernel,
        out_shape=jax.ShapeDtypeStruct((chips, per, n_obs), BF16),
        in_specs=[VMEM] * 3,
        out_specs=VMEM,
        compiler_params=limit(8),
        name="observe",
    )(ensemble, obs_weight, obs_column.reshape(1, n_obs))
    seen = lax.all_to_all(seen, "member", 0, 0, axis_index_groups=same_core, tiled=True)
    seen_too = permute(seen, swap)

    trans = pl.pallas_call(
        transform_kernel,
        out_shape=jax.ShapeDtypeStruct((count, per, count * per), BF16),
        in_specs=[SMEM] + [VMEM] * 5,
        out_specs=VMEM,
        scratch_shapes=[
            pltpu.VMEM((count * per, n_obs), BF16),
            pltpu.VMEM((2, count * per + 16, n_obs), BF16),
        ],
        compiler_params=limit(8),
        name="transform",
    )(
        where,
        seen,
        seen_too,
        obs_value.reshape(n_obs // 128, 128),
        obs_rinv.reshape(n_obs // 128, 128),
        set_rows,
    )
    trans = lax.all_to_all(trans, "member", 0, 0, tiled=True)

    return pl.pallas_call(
        apply_kernel,
        out_shape=jax.ShapeDtypeStruct((per, nv, cols), F32),
        in_specs=[SMEM] + [VMEM] * (3 + len(blocks)),
        out_specs=pl.BlockSpec(memory_space=pl.ANY),
        scratch_shapes=[
            pltpu.VMEM((count * per + 16, count * per), BF16),
            pltpu.VMEM((per, nv, cols), F32),
            pltpu.SemaphoreType.DMA((4,)),
        ],
        compiler_params=limit(4),
        name="apply",
    )(where, trans, neighbour, interp_weight, *blocks)


def solution(mesh):
    placed = (
        P("member", None, "space"),
        P(None, "space"),
        P("space"),
        P("space"),
        P("space"),
        P("space", None),
        P("space"),
        P(None, "space"),
        P(None, "space"),
    )
    return jax.shard_map(
        analysis, mesh=mesh, in_specs=placed, out_specs=P("member", None, "space"), check_vma=False
    )
```
